32 devices in a mesh: fsdp: 32 (over z, y, x, core).
Axes of the slice: x: 2, y: 2, z: 4, core: 2. Of those that a mesh axis runs over, the one named last changes fastest.
Arguments:
- block_input: bfloat16 [8192, 1024], P('fsdp'), may hold values from -6 to 6
- seq_start: int32 [8192], P('fsdp'), may hold values from 0 to 255, as said below
- fill_count: int32 [32], P('fsdp'), may hold values from 64 to 256, as said below
- w_qkv: bfloat16 [1024, 3072], P('fsdp')
- w_dense: bfloat16 [1024, 1024], P('fsdp'), may hold values from -0.75 to 0.75
- w_fc1: bfloat16 [1024, 4096], P('fsdp'), may hold values from -0.1875 to 0.1875
- w_fc2: bfloat16 [4096, 1024], P('fsdp'), may hold values from -0.09375 to 0.09375
- b_qkv: bfloat16 [3072], P('fsdp'), may hold values from -3 to 3
- b_dense: bfloat16 [1024], P('fsdp'), may hold values from -2 to 2
- b_fc1: bfloat16 [4096], P('fsdp'), may hold values from -3 to 3
- b_fc2: bfloat16 [1024], P('fsdp'), may hold values from -2 to 2
- ln1_gain: bfloat16 [1024], P('fsdp'), may hold values from 0.5 to 1.5
- ln1_bias: bfloat16 [1024], P('fsdp'), may hold values from -2 to 2
- ln2_gain: bfloat16 [1024], P('fsdp'), may hold values from 0.5 to 1.5
- ln2_bias: bfloat16 [1024], P('fsdp'), may hold values from -2 to 2
- cotangent: float32 [8192, 1024], P('fsdp'), may hold values from -6 to 6
Outputs:
- block_output: bfloat16 [8192, 1024], P('fsdp')
- input_grad: float32 [8192, 1024], P('fsdp')
- grad_w_qkv: float32 [1024, 3072], P('fsdp')
- grad_w_dense: float32 [1024, 1024], P('fsdp')
- grad_w_fc1: float32 [1024, 4096], P('fsdp')
- grad_w_fc2: float32 [4096, 1024], P('fsdp')
- grad_b_qkv: float32 [3072], P('fsdp')
- grad_b_dense: float32 [1024], P('fsdp')
- grad_b_fc1: float32 [4096], P('fsdp')
- grad_b_fc2: float32 [1024], P('fsdp')
- grad_ln1_gain: float32 [1024], P('fsdp')
- grad_ln1_bias: float32 [1024], P('fsdp')
- grad_ln2_gain: float32 [1024], P('fsdp')
- grad_ln2_bias: float32 [1024], P('fsdp')
The draws below stay inside these ranges and needn't reach their ends.
Inputs may be any that keep to these rules, and one draw needn't show every extreme that they name: Sequences never cross devices; for each row, seq_start is at most the row's own index within its device, and all rows of one sequence share it and follow one another; rows at or beyond their device's fill_count start at themselves. The live rows of each device are its first fill_count rows.
All inputs are finite; a program needn't handle non-finite values.
Results may differ from the reference program's by a relative error of at most 0.01.
Values may be sent and summed in bfloat16 or wider, within the bound.
A program may use at most 192 MiB of HBM per device.

```python
import math
import jax
import jax.numpy as jnp
from jax import lax

D = 1024
HEAD_DIM = 64
ROT = 16
FF = 4096
TOK_DEV = 256
TOKENS = 8192
N_FSDP = 32


def layout_draw(key):
    fill_key, full_key, flag_key = jax.random.split(jax.random.fold_in(key, 7), 3)
    fills = jax.random.randint(fill_key, (N_FSDP,), TOK_DEV // 4, TOK_DEV + 1)
    full_device = jax.random.randint(full_key, (), 0, N_FSDP)
    device_index = jnp.arange(N_FSDP, dtype=jnp.int32)
    fills = jnp.where(device_index == full_device, TOK_DEV, fills)
    fills = jnp.where(device_index == (full_device + 1) % N_FSDP, TOK_DEV // 4, fills)
    flags = jax.random.randint(flag_key, (N_FSDP, TOK_DEV), 0, 40) == 0
    row_index = jnp.arange(TOK_DEV, dtype=jnp.int32)[None, :]
    live_rows = row_index < fills[:, None]
    begins = flags | (row_index == 0) | jnp.logical_not(live_rows)
    marked = jnp.where(begins, row_index, 0)
    starts = lax.cummax(marked, axis=1)
    return (fills.astype(jnp.int32), starts.reshape(N_FSDP * TOK_DEV).astype(jnp.int32))


def draw_seq_start(key, part):
    return layout_draw(key)[1]


def draw_fill_count(key, part):
    return layout_draw(key)[0]


def draw_w_qkv(key, part):
    base_key = jax.random.fold_in(jax.random.fold_in(key, 11), 0)
    weights_all = jax.random.normal(base_key, (D, 3 * D), jnp.float32) * D ** (-0.5)
    return weights_all.astype(jnp.bfloat16)


def levels(own_key, extent, shards, low, high):
    def one(axis_at, shards_of):
        steps = jax.random.uniform(jax.random.fold_in(jax.random.fold_in(own_key, 6), axis_at), (shards_of,), jnp.float32, low / len(shards), high / len(shards))
        return jnp.repeat(jnp.exp(steps), extent[axis_at] // shards_of).reshape((-1,) + (1,) * (len(extent) - axis_at - 1))

    factor_of = one(*shards[0])
    for cut in shards[1:]:
        factor_of = factor_of * one(*cut)
    return factor_of


def noise(key, shape, spread, reach, cuts=(), kind=jnp.bfloat16):
    result = spread * jax.random.normal(key, shape, jnp.float32)
    if cuts:
        result = result * levels(key, shape, cuts, -0.22, 0.18)
    return jnp.clip(result, -reach, reach).astype(kind)


def setup_inputs(seed: int = 0) -> dict:
    key_of = jax.random.split(jax.random.key(seed), 17)
    block_input = noise(key_of[0], (TOKENS, D), 1.0, 6.0, ((0, 32),))
    seq_start = draw_seq_start(jax.random.fold_in(key_of[16], 71), 0)
    fill_count = draw_fill_count(jax.random.fold_in(key_of[16], 71), 0)
    w_qkv = draw_w_qkv(jax.random.fold_in(key_of[16], 71), 0)
    w_dense = noise(key_of[4], (D, D), (D // 16) ** -0.5, 0.75, ((0, 32),))
    w_fc1 = noise(key_of[5], (D, FF), D ** -0.5, 0.1875, ((0, 32),))
    w_fc2 = noise(key_of[6], (FF, D), FF ** -0.5, 0.09375, ((0, 32),))
    b_qkv = noise(key_of[7], (3 * D,), 0.5, 3.0, ((0, 32),))
    b_dense = noise(key_of[8], (D,), 0.3, 2.0, ((0, 32),))
    b_fc1 = noise(key_of[9], (FF,), 0.5, 3.0, ((0, 32),))
    b_fc2 = noise(key_of[10], (D,), 0.3, 2.0, ((0, 32),))
    ln1_gain = jnp.clip(1.0 + 0.1 * jax.random.normal(key_of[11], (D,), jnp.float32), 0.5, 1.5).astype(jnp.bfloat16)
    ln1_bias = noise(key_of[12], (D,), 0.3, 2.0, ((0, 32),))
    ln2_gain = jnp.clip(1.0 + 0.1 * jax.random.normal(key_of[13], (D,), jnp.float32), 0.5, 1.5).astype(jnp.bfloat16)
    ln2_bias = noise(key_of[14], (D,), 0.3, 2.0, ((0, 32),))
    cotangent = noise(key_of[15], (TOKENS, D), 1.0, 6.0, ((0, 32),), jnp.float32)
    return dict(block_input=block_input, seq_start=seq_start, fill_count=fill_count, w_qkv=w_qkv, w_dense=w_dense, w_fc1=w_fc1, w_fc2=w_fc2, b_qkv=b_qkv, b_dense=b_dense, b_fc1=b_fc1, b_fc2=b_fc2, ln1_gain=ln1_gain, ln1_bias=ln1_bias, ln2_gain=ln2_gain, ln2_bias=ln2_bias, cotangent=cotangent)


epsilon = 1e-05
masked_value = -1e+30

def matmul(left_arg, right_arg):
    return jnp.dot(left_arg, right_arg, preferred_element_type=jnp.float32)

def product(pattern, left_arg, right_arg):
    return jnp.einsum(pattern, left_arg.astype(jnp.float32), right_arg.astype(jnp.float32))

def normalize(input_rows):
    mean_value = lax.optimization_barrier(jnp.mean(input_rows, axis=-1, keepdims=True))
    centered = input_rows - mean_value
    inv_std = lax.rsqrt(lax.optimization_barrier(jnp.mean(centered * centered, axis=-1, keepdims=True)) + epsilon)
    return (centered * inv_std, inv_std)

def rotary_tables(starts, row_count):
    position = (jnp.arange(row_count, dtype=jnp.int32) - starts).astype(jnp.float32)
    half_rot = ROT // 2
    frequency = jnp.exp(jnp.arange(half_rot, dtype=jnp.float32) * (-2.0 * math.log(10000.0) / ROT))
    angles = position[:, None] * frequency[None, :]
    return (jnp.cos(angles)[:, None, :], jnp.sin(angles)[:, None, :])

def rotate(tensor, cosine_table, sine_table, orient):
    half_rot = ROT // 2
    lower_half = tensor[..., :half_rot]
    upper_half = tensor[..., half_rot:ROT]
    new_lower = lower_half * cosine_table - orient * upper_half * sine_table
    new_upper = upper_half * cosine_table + orient * lower_half * sine_table
    return jnp.concatenate([new_lower, new_upper, tensor[..., ROT:]], axis=-1)

def gelu_parts(pre_act):
    normal_cdf = 0.5 * (1.0 + lax.erf(pre_act * (1.0 / math.sqrt(2.0))))
    activated = pre_act * normal_cdf
    derivative = normal_cdf + pre_act * jnp.exp(-0.5 * pre_act * pre_act) * (1.0 / math.sqrt(2.0 * math.pi))
    return (activated, derivative)

def allowed_pairs(starts, row_count):
    row_index = jnp.arange(row_count, dtype=jnp.int32)
    return (row_index[None, :] <= row_index[:, None]) & (row_index[None, :] >= starts[:, None])

def attention_scores(query_rot, key_rot, allowed):
    scores = product('qhd,khd->hqk', query_rot, key_rot) * HEAD_DIM ** (-0.5)
    return jnp.where(allowed[None], scores, masked_value)

def forward_rows(block_rows, starts, params):
    w_qkv, w_dense, w_fc1, w_fc2, b_qkv, b_dense, b_fc1, b_fc2, gain_one, bias_one, gain_two, bias_two = params
    row_count, model_width = block_rows.shape
    head_count = model_width // HEAD_DIM
    input_f32 = block_rows.astype(jnp.float32)
    normed, inv_std = normalize(input_f32)
    hidden_one = (normed * gain_one.astype(jnp.float32) + bias_one.astype(jnp.float32)).astype(jnp.bfloat16)
    hidden_two = (normed * gain_two.astype(jnp.float32) + bias_two.astype(jnp.float32)).astype(jnp.bfloat16)
    projected = matmul(hidden_one, w_qkv) + b_qkv.astype(jnp.float32)
    queries = projected[:, :model_width].reshape(row_count, head_count, HEAD_DIM)
    keys_all = projected[:, model_width:2 * model_width].reshape(row_count, head_count, HEAD_DIM)
    values_all = projected[:, 2 * model_width:].reshape(row_count, head_count, HEAD_DIM)
    cosine_table, sine_table = rotary_tables(starts, row_count)
    query_rot = rotate(queries, cosine_table, sine_table, 1.0).astype(jnp.bfloat16)
    key_rot = rotate(keys_all, cosine_table, sine_table, 1.0).astype(jnp.bfloat16)
    value_b = values_all.astype(jnp.bfloat16)
    allowed = allowed_pairs(starts, row_count)
    scores = attention_scores(query_rot, key_rot, allowed)
    row_max = lax.optimization_barrier(jnp.max(scores, axis=-1, keepdims=True))
    log_total = row_max + jnp.log(lax.optimization_barrier(jnp.sum(jnp.exp(scores - row_max), axis=-1, keepdims=True)))
    weights_b = jnp.exp(scores - log_total).astype(jnp.bfloat16)
    context = product('hqk,khd->qhd', weights_b, value_b).reshape(row_count, model_width).astype(jnp.bfloat16)
    attn_out = matmul(context, w_dense) + b_dense.astype(jnp.float32)
    pre_act = matmul(hidden_two, w_fc1) + b_fc1.astype(jnp.float32)
    activated, derivative = gelu_parts(pre_act)
    act_b = activated.astype(jnp.bfloat16)
    mlp_out = matmul(act_b, w_fc2) + b_fc2.astype(jnp.float32)
    block_output = (input_f32 + attn_out + mlp_out).astype(jnp.bfloat16)
    kept_state = (normed, inv_std, hidden_one, hidden_two, query_rot, key_rot, value_b, log_total, context, derivative, act_b, cosine_table, sine_table, allowed)
    return (block_output, kept_state)

def norm_back(d_hidden, normed, inv_std, gain_param):
    d_normed = d_hidden * gain_param.astype(jnp.float32)
    grad_gain = lax.optimization_barrier(jnp.sum(d_hidden * normed, axis=0))
    grad_bias = lax.optimization_barrier(jnp.sum(d_hidden, axis=0))
    mean_one = lax.optimization_barrier(jnp.mean(d_normed, axis=-1, keepdims=True))
    mean_two = lax.optimization_barrier(jnp.mean(d_normed * normed, axis=-1, keepdims=True))
    return (inv_std * (d_normed - mean_one - normed * mean_two), grad_gain, grad_bias)

def backward_mlp(grad_rows, kept_state, params):
    w_qkv, w_dense, w_fc1, w_fc2, b_qkv, b_dense, b_fc1, b_fc2, gain_one, bias_one, gain_two, bias_two = params
    normed, inv_std, hidden_one, hidden_two = (kept_state[0], kept_state[1], kept_state[2], kept_state[3])
    derivative, act_b = (kept_state[9], kept_state[10])
    grad_b = grad_rows.astype(jnp.bfloat16)
    grad_w_fc2 = matmul(act_b.T, grad_b)
    grad_b_fc2 = lax.optimization_barrier(jnp.sum(grad_rows, axis=0))
    d_pre = matmul(grad_b, w_fc2.T) * derivative
    grad_b_fc1 = lax.optimization_barrier(jnp.sum(d_pre, axis=0))
    d_pre_b = d_pre.astype(jnp.bfloat16)
    grad_w_fc1 = matmul(hidden_two.T, d_pre_b)
    d_hidden_two = matmul(d_pre_b, w_fc1.T)
    dx_two, grad_gain_two, grad_bias_two = norm_back(d_hidden_two, normed, inv_std, gain_two)
    return ((grad_w_fc1, grad_w_fc2, grad_b_fc1, grad_b_fc2, grad_gain_two, grad_bias_two), dx_two)

def backward_attention(grad_rows, kept_state, params):
    w_qkv, w_dense, w_fc1, w_fc2, b_qkv, b_dense, b_fc1, b_fc2, gain_one, bias_one, gain_two, bias_two = params
    normed, inv_std, hidden_one, hidden_two, query_rot, key_rot, value_b, log_total, context, derivative, act_b, cosine_table, sine_table, allowed = kept_state
    row_count, model_width = context.shape
    head_count = model_width // HEAD_DIM
    grad_b = grad_rows.astype(jnp.bfloat16)
    grad_w_dense = matmul(context.T, grad_b)
    grad_b_dense = lax.optimization_barrier(jnp.sum(grad_rows, axis=0))
    d_context = matmul(grad_b, w_dense.T).astype(jnp.bfloat16).reshape(row_count, head_count, HEAD_DIM)
    scores = attention_scores(query_rot, key_rot, allowed)
    probabilities = jnp.exp(scores - log_total)
    probs_b = probabilities.astype(jnp.bfloat16)
    d_value = product('hqk,qhd->khd', probs_b, d_context)
    d_probs = product('qhd,khd->hqk', d_context, value_b)
    row_delta = lax.optimization_barrier(jnp.sum(d_context.astype(jnp.float32) * context.reshape(row_count, head_count, HEAD_DIM).astype(jnp.float32), axis=-1))
    d_scores = (probabilities * (d_probs - jnp.transpose(row_delta)[:, :, None])).astype(jnp.bfloat16)
    d_query_rot = product('hqk,khd->qhd', d_scores, key_rot) * HEAD_DIM ** (-0.5)
    d_key_rot = product('hqk,qhd->khd', d_scores, query_rot) * HEAD_DIM ** (-0.5)
    d_queries = rotate(d_query_rot, cosine_table, sine_table, -1.0)
    d_keys = rotate(d_key_rot, cosine_table, sine_table, -1.0)
    d_projected = jnp.concatenate([d_queries.reshape(row_count, model_width), d_keys.reshape(row_count, model_width), d_value.reshape(row_count, model_width)], axis=1)
    grad_b_qkv = lax.optimization_barrier(jnp.sum(d_projected, axis=0))
    d_projected_b = d_projected.astype(jnp.bfloat16)
    grad_w_qkv = matmul(hidden_one.T, d_projected_b)
    d_hidden_one = matmul(d_projected_b, w_qkv.T)
    dx_one, grad_gain_one, grad_bias_one = norm_back(d_hidden_one, normed, inv_std, gain_one)
    return ((grad_w_qkv, grad_w_dense, grad_b_qkv, grad_b_dense, grad_gain_one, grad_bias_one), dx_one)

def arrange(attn_grads, mlp_grads):
    return (attn_grads[0], attn_grads[1], mlp_grads[0], mlp_grads[1], attn_grads[2], attn_grads[3], mlp_grads[2], mlp_grads[3], attn_grads[4], attn_grads[5], mlp_grads[4], mlp_grads[5])

def reference(block_input, seq_start, fill_count, w_qkv, w_dense, w_fc1, w_fc2, b_qkv, b_dense, b_fc1, b_fc2, ln1_gain, ln1_bias, ln2_gain, ln2_bias, cotangent):
    params = (w_qkv, w_dense, w_fc1, w_fc2, b_qkv, b_dense, b_fc1, b_fc2, ln1_gain, ln1_bias, ln2_gain, ln2_bias)
    input_blocks = block_input.reshape(N_FSDP, TOK_DEV, D)
    start_blocks = seq_start.reshape(N_FSDP, TOK_DEV)
    grad_blocks = cotangent.reshape(N_FSDP, TOK_DEV, D)

    def one_device(totals, pieces):
        rows_block, starts, fill_one, grad_block = pieces
        live_rows = jnp.arange(TOK_DEV, dtype=jnp.int32) < fill_one
        grad_live = jnp.where(live_rows[:, None], grad_block, jnp.float32(0.0))
        output_rows, kept_state = forward_rows(rows_block, starts, params)
        mlp_grads, dx_two = backward_mlp(grad_live, kept_state, params)
        attn_grads, dx_one = backward_attention(grad_live, kept_state, params)
        ordered = arrange(attn_grads, mlp_grads)
        totals = tuple((total + piece for total, piece in zip(totals, ordered)))
        return (totals, (output_rows, grad_live + dx_one + dx_two))
    initial = tuple((jnp.zeros(param.shape, jnp.float32) for param in params))
    totals, (outputs, input_grads) = lax.scan(one_device, initial, (input_blocks, start_blocks, fill_count, grad_blocks))
    return (outputs.reshape(TOKENS, D), input_grads.reshape(TOKENS, D), totals[0], totals[1], totals[2], totals[3], totals[4], totals[5], totals[6], totals[7], totals[8], totals[9], totals[10], totals[11])
```

```python
import math

import jax
import jax.numpy as jnp
from jax import lax
from jax.sharding import PartitionSpec as P

HEAD_DIM = 64
ROT = 16


epsilon = 1e-05
masked_value = -1e30


def matmul(left_arg, right_arg):
    return jnp.dot(left_arg, right_arg, preferred_element_type=jnp.float32)


def product(pattern, left_arg, right_arg):
    return jnp.einsum(pattern, left_arg, right_arg, preferred_element_type=jnp.float32)


def stage_orders(device_count):
    bit_count = device_count.bit_length() - 1
    high = list(range(bit_count - 1, 2, -1))
    low = [bit for bit in (1, 2) if bit < bit_count]
    return (high + low + [0], high + low[::-1] + [0])


def swap_bit(array, bit):
    device_count = lax.axis_size("fsdp")
    pairs = [(index, index ^ (1 << bit)) for index in range(device_count)]
    return lax.ppermute(array, "fsdp", pairs)


def own_bit(bit):
    return (lax.axis_index("fsdp") // (1 << bit)) % 2


def grow(block, order):
    done = []
    for bit in order:
        done = sorted(done + [bit], reverse=True)
        axis = done.index(bit)
        other = swap_bit(block, bit)
        mine_low = own_bit(bit) == 0
        low = jnp.where(mine_low, block, other)
        high = jnp.where(mine_low, other, block)
        block = jnp.stack([low, high], axis=axis)
    return block


def gather_rows(shard):
    device_count = lax.axis_size("fsdp")
    order_one, order_two = stage_orders(device_count)
    rows, columns = shard.shape
    if columns % 256:
        return grow(shard, order_one).reshape(device_count * rows, columns)
    half = columns // 2
    parts = [grow(shard[:, :half], order_one), grow(shard[:, half:], order_two)]
    return jnp.concatenate(
        [part.reshape(device_count * rows, half) for part in parts], axis=1
    )


def gather_small(vector):
    device_count = lax.axis_size("fsdp")
    return grow(vector, stage_orders(device_count)[0]).reshape(device_count, -1)


def shrink(block, bits, order, wire):
    left = list(bits)
    for bit in order:
        axis = left.index(bit)
        left.remove(bit)
        mine = own_bit(bit)
        send = lax.dynamic_index_in_dim(block, 1 - mine, axis, keepdims=False)
        keep = lax.dynamic_index_in_dim(block, mine, axis, keepdims=False)
        block = keep + swap_bit(send.astype(wire), bit).astype(jnp.float32)
    return block


def scatter_small(block):
    device_count, width = block.shape
    bit_count = device_count.bit_length() - 1
    order = stage_orders(device_count)[0][::-1]
    bits = list(range(bit_count - 1, -1, -1))
    return shrink(block.reshape((2,) * bit_count + (width,)), bits, order, jnp.float32)


def grad_shard(left_arg, right_arg):
    device_count = lax.axis_size("fsdp")
    bit_count = device_count.bit_length() - 1
    row_count, width = left_arg.shape
    rows = width // device_count
    columns = right_arg.shape[1]
    by_core = left_arg.reshape(row_count, device_count // 2, 2, rows)
    mine = own_bit(0)
    pick = lambda which: lax.dynamic_index_in_dim(by_core, which, 2, keepdims=False).reshape(
        row_count, width // 2
    )
    away = matmul(pick(1 - mine).T, right_arg).astype(jnp.bfloat16)
    orders = [order[::-1][1:] for order in stage_orders(device_count)]
    bits = list(range(bit_count - 1, 0, -1))
    arrived = swap_bit(away, 0).astype(jnp.float32)
    total = matmul(pick(mine).T, right_arg) + arrived
    half = columns // 2
    parts = []
    for order, part in zip(orders, (total[:, :half], total[:, half:])):
        part = part.reshape((2,) * (bit_count - 1) + (rows, half))
        parts.append(shrink(part, bits, order, jnp.bfloat16))
    return jnp.concatenate(parts, axis=1)


def normalize(input_rows):
    mean_value = jnp.mean(input_rows, axis=-1, keepdims=True)
    centered = input_rows - mean_value
    inv_std = lax.rsqrt(jnp.mean(centered * centered, axis=-1, keepdims=True) + epsilon)
    return (centered * inv_std, inv_std)


def rotary_tables(starts, row_count):
    position = (jnp.arange(row_count, dtype=jnp.int32) - starts).astype(jnp.float32)
    half_rot = ROT // 2
    frequency = jnp.exp(jnp.arange(half_rot, dtype=jnp.float32) * (-2.0 * math.log(10000.0) / ROT))
    angles = position[:, None] * frequency[None, :]
    return (jnp.cos(angles)[:, None, :], jnp.sin(angles)[:, None, :])


def rotate(tensor, cosine_table, sine_table, orient):
    half_rot = ROT // 2
    lower_half = tensor[..., :half_rot]
    upper_half = tensor[..., half_rot:ROT]
    new_lower = lower_half * cosine_table - orient * upper_half * sine_table
    new_upper = upper_half * cosine_table + orient * lower_half * sine_table
    return jnp.concatenate([new_lower, new_upper, tensor[..., ROT:]], axis=-1)


def gelu_parts(pre_act):
    normal_cdf = 0.5 * (1.0 + lax.erf(pre_act * (1.0 / math.sqrt(2.0))))
    activated = pre_act * normal_cdf
    derivative = normal_cdf + pre_act * jnp.exp(-0.5 * pre_act * pre_act) * (
        1.0 / math.sqrt(2.0 * math.pi)
    )
    return (activated, derivative)


def allowed_pairs(starts, row_count):
    row_index = jnp.arange(row_count, dtype=jnp.int32)
    return (row_index[None, :] <= row_index[:, None]) & (row_index[None, :] >= starts[:, None])


def attention_scores(query_rot, key_rot, allowed):
    scores = product("qhd,khd->hqk", query_rot, key_rot) * HEAD_DIM ** (-0.5)
    return jnp.where(allowed[None], scores, masked_value)


def forward_rows(block_rows, starts, params):
    (
        w_qkv,
        w_dense,
        w_fc1,
        w_fc2,
        b_qkv,
        b_dense,
        b_fc1,
        b_fc2,
        gain_one,
        bias_one,
        gain_two,
        bias_two,
    ) = params
    row_count, model_width = block_rows.shape
    head_count = model_width // HEAD_DIM
    input_f32 = block_rows.astype(jnp.float32)
    normed, inv_std = normalize(input_f32)
    hidden_one = (normed * gain_one.astype(jnp.float32) + bias_one.astype(jnp.float32)).astype(
        jnp.bfloat16
    )
    hidden_two = (normed * gain_two.astype(jnp.float32) + bias_two.astype(jnp.float32)).astype(
        jnp.bfloat16
    )
    projected = matmul(hidden_one, w_qkv) + b_qkv.astype(jnp.float32)
    queries = projected[:, :model_width].reshape(row_count, head_count, HEAD_DIM)
    keys_all = projected[:, model_width : 2 * model_width].reshape(row_count, head_count, HEAD_DIM)
    values_all = projected[:, 2 * model_width :].reshape(row_count, head_count, HEAD_DIM)
    cosine_table, sine_table = rotary_tables(starts, row_count)
    query_rot = rotate(queries, cosine_table, sine_table, 1.0).astype(jnp.bfloat16)
    key_rot = rotate(keys_all, cosine_table, sine_table, 1.0).astype(jnp.bfloat16)
    value_b = values_all.astype(jnp.bfloat16)
    allowed = allowed_pairs(starts, row_count)
    scores = attention_scores(query_rot, key_rot, allowed)
    row_max = jnp.max(scores, axis=-1, keepdims=True)
    log_total = row_max + jnp.log(jnp.sum(jnp.exp(scores - row_max), axis=-1, keepdims=True))
    weights_b = jnp.exp(scores - log_total).astype(jnp.bfloat16)
    context = (
        product("hqk,khd->qhd", weights_b, value_b)
        .reshape(row_count, model_width)
        .astype(jnp.bfloat16)
    )
    attn_out = matmul(context, w_dense) + b_dense.astype(jnp.float32)
    pre_act = matmul(hidden_two, w_fc1) + b_fc1.astype(jnp.float32)
    activated, derivative = gelu_parts(pre_act)
    act_b = activated.astype(jnp.bfloat16)
    mlp_out = matmul(act_b, w_fc2) + b_fc2.astype(jnp.float32)
    block_output = (input_f32 + attn_out + mlp_out).astype(jnp.bfloat16)
    kept_state = (
        normed,
        inv_std,
        hidden_one,
        hidden_two,
        query_rot,
        key_rot,
        value_b,
        log_total,
        context,
        derivative,
        act_b,
        cosine_table,
        sine_table,
        allowed,
    )
    return (block_output, kept_state)


def norm_back(d_hidden, normed, inv_std, gain_param):
    d_normed = d_hidden * gain_param.astype(jnp.float32)
    grad_gain = jnp.sum(d_hidden * normed, axis=0)
    grad_bias = jnp.sum(d_hidden, axis=0)
    mean_one = jnp.mean(d_normed, axis=-1, keepdims=True)
    mean_two = jnp.mean(d_normed * normed, axis=-1, keepdims=True)
    return (inv_std * (d_normed - mean_one - normed * mean_two), grad_gain, grad_bias)


def backward_mlp(grad_rows, kept_state, params):
    (
        w_qkv,
        w_dense,
        w_fc1,
        w_fc2,
        b_qkv,
        b_dense,
        b_fc1,
        b_fc2,
        gain_one,
        bias_one,
        gain_two,
        bias_two,
    ) = params
    normed, inv_std, hidden_one, hidden_two = (
        kept_state[0],
        kept_state[1],
        kept_state[2],
        kept_state[3],
    )
    derivative, act_b = (kept_state[9], kept_state[10])
    grad_b = grad_rows.astype(jnp.bfloat16)
    grad_w_fc2 = grad_shard(act_b, grad_b)
    grad_b_fc2 = jnp.sum(grad_rows, axis=0)
    d_pre = matmul(grad_b, w_fc2.T) * derivative
    grad_b_fc1 = jnp.sum(d_pre, axis=0)
    d_pre_b = d_pre.astype(jnp.bfloat16)
    grad_w_fc1 = grad_shard(hidden_two, d_pre_b)
    d_hidden_two = matmul(d_pre_b, w_fc1.T)
    dx_two, grad_gain_two, grad_bias_two = norm_back(d_hidden_two, normed, inv_std, gain_two)
    return ((grad_w_fc1, grad_w_fc2, grad_b_fc1, grad_b_fc2, grad_gain_two, grad_bias_two), dx_two)


def backward_attention(grad_rows, kept_state, params):
    (
        w_qkv,
        w_dense,
        w_fc1,
        w_fc2,
        b_qkv,
        b_dense,
        b_fc1,
        b_fc2,
        gain_one,
        bias_one,
        gain_two,
        bias_two,
    ) = params
    (
        normed,
        inv_std,
        hidden_one,
        hidden_two,
        query_rot,
        key_rot,
        value_b,
        log_total,
        context,
        derivative,
        act_b,
        cosine_table,
        sine_table,
        allowed,
    ) = kept_state
    row_count, model_width = context.shape
    head_count = model_width // HEAD_DIM
    grad_b = grad_rows.astype(jnp.bfloat16)
    grad_w_dense = grad_shard(context, grad_b)
    grad_b_dense = jnp.sum(grad_rows, axis=0)
    d_context = (
        matmul(grad_b, w_dense.T).astype(jnp.bfloat16).reshape(row_count, head_count, HEAD_DIM)
    )
    scores = attention_scores(query_rot, key_rot, allowed)
    probabilities = jnp.exp(scores - log_total)
    probs_b = probabilities.astype(jnp.bfloat16)
    d_value = product("hqk,qhd->khd", probs_b, d_context)
    d_probs = product("qhd,khd->hqk", d_context, value_b)
    row_delta = jnp.sum(
        d_context.astype(jnp.float32)
        * context.reshape(row_count, head_count, HEAD_DIM).astype(jnp.float32),
        axis=-1,
    )
    d_scores = (probabilities * (d_probs - jnp.transpose(row_delta)[:, :, None])).astype(
        jnp.bfloat16
    )
    d_query_rot = product("hqk,khd->qhd", d_scores, key_rot) * HEAD_DIM ** (-0.5)
    d_key_rot = product("hqk,qhd->khd", d_scores, query_rot) * HEAD_DIM ** (-0.5)
    d_queries = rotate(d_query_rot, cosine_table, sine_table, -1.0)
    d_keys = rotate(d_key_rot, cosine_table, sine_table, -1.0)
    d_projected = jnp.concatenate(
        [
            d_queries.reshape(row_count, model_width),
            d_keys.reshape(row_count, model_width),
            d_value.reshape(row_count, model_width),
        ],
        axis=1,
    )
    grad_b_qkv = jnp.sum(d_projected, axis=0)
    d_projected_b = d_projected.astype(jnp.bfloat16)
    grad_w_qkv = grad_shard(hidden_one, d_projected_b)
    d_hidden_one = matmul(d_projected_b, w_qkv.T)
    dx_one, grad_gain_one, grad_bias_one = norm_back(d_hidden_one, normed, inv_std, gain_one)
    return (
        (grad_w_qkv, grad_w_dense, grad_b_qkv, grad_b_dense, grad_gain_one, grad_bias_one),
        dx_one,
    )


def arrange(attn_grads, mlp_grads):
    return (
        attn_grads[0],
        attn_grads[1],
        mlp_grads[0],
        mlp_grads[1],
        attn_grads[2],
        attn_grads[3],
        mlp_grads[2],
        mlp_grads[3],
        attn_grads[4],
        attn_grads[5],
        mlp_grads[4],
        mlp_grads[5],
    )


def per_device(
    block_input,
    seq_start,
    fill_count,
    w_qkv,
    w_dense,
    w_fc1,
    w_fc2,
    b_qkv,
    b_dense,
    b_fc1,
    b_fc2,
    ln1_gain,
    ln1_bias,
    ln2_gain,
    ln2_bias,
    cotangent,
):
    device_count = lax.axis_size("fsdp")
    small = (b_qkv, b_dense, b_fc1, b_fc2, ln1_gain, ln1_bias, ln2_gain, ln2_bias)
    widths = [array.shape[0] for array in small]
    packed = gather_small(jnp.concatenate(small))
    vectors = []
    begin = 0
    for width in widths:
        vectors.append(packed[:, begin : begin + width].reshape(device_count * width))
        begin += width
    full_fc1 = gather_rows(w_fc1)
    full_fc2 = gather_rows(w_fc2)
    full_qkv = gather_rows(w_qkv)
    full_dense = gather_rows(w_dense)
    params = (full_qkv, full_dense, full_fc1, full_fc2) + tuple(vectors)
    block_output, kept_state = forward_rows(block_input, seq_start, params)
    row_count = block_input.shape[0]
    live_rows = jnp.arange(row_count, dtype=jnp.int32) < fill_count[0]
    grad_live = jnp.where(live_rows[:, None], cotangent, jnp.float32(0.0))
    mlp_grads, dx_two = backward_mlp(grad_live, kept_state, params)
    attn_grads, dx_one = backward_attention(grad_live, kept_state, params)
    ordered = arrange(attn_grads, mlp_grads)
    packed_grads = scatter_small(
        jnp.concatenate([vector.reshape(device_count, -1) for vector in ordered[4:]], axis=1)
    )
    pieces = []
    begin = 0
    for width in widths:
        pieces.append(packed_grads[begin : begin + width])
        begin += width
    shares = tuple(ordered[:4]) + tuple(pieces)
    input_grad = grad_live + dx_one + dx_two
    return (
        block_output,
        input_grad,
        shares[0],
        shares[1],
        shares[2],
        shares[3],
        shares[4],
        shares[5],
        shares[6],
        shares[7],
        shares[8],
        shares[9],
        shares[10],
        shares[11],
    )


def solution(mesh):
    in_specs = (
        P("fsdp", None),
        P("fsdp"),
        P("fsdp"),
        P("fsdp", None),
        P("fsdp", None),
        P("fsdp", None),
        P("fsdp", None),
        P("fsdp"),
        P("fsdp"),
        P("fsdp"),
        P("fsdp"),
        P("fsdp"),
        P("fsdp"),
        P("fsdp"),
        P("fsdp"),
        P("fsdp", None),
    )
    out_specs = (
        P("fsdp", None),
        P("fsdp", None),
        P("fsdp", None),
        P("fsdp", None),
        P("fsdp", None),
        P("fsdp", None),
        P("fsdp"),
        P("fsdp"),
        P("fsdp"),
        P("fsdp"),
        P("fsdp"),
        P("fsdp"),
        P("fsdp"),
        P("fsdp"),
    )
    return jax.shard_map(
        per_device, mesh=mesh, in_specs=in_specs, out_specs=out_specs, check_vma=False
    )
```
